256 devices in a mesh: gx: 64 (over y, x, z_lo), gy: 4 (over z_hi, core).
Axes of the slice: x: 4, y: 4, z: 8 (z_hi: 2, z_lo: 4; z = z_hi * 4 + z_lo), core: 2. Of those that a mesh axis runs over, the one named last changes fastest.
Arguments:
- fractions: float32 [3, 131072], P(None, ('gx', 'gy')), may hold values from 0 to 1
- species: int32 [131072], P(('gx', 'gy')), may hold values from 0 to 5
- send_list: int32 [8, 4096], P(None, ('gx', 'gy')), may hold values from 0 to 511
- tile_list: int32 [2, 1536], P(None, ('gx', 'gy')), may hold values from 0 to 9, as said below
- counts: int32 [256], P(('gx', 'gy')), may hold values from 2 to 6, as said below
- embedding: float32 [6, 128], replicated, may hold values from -6 to 6
- radial: float32 [4, 8, 128], replicated, may hold values from -0.75 to 0.75
- mixing: float32 [5, 128, 128], replicated, may hold values from -0.5 to 0.5
- readout: float32 [128], replicated, may hold values from -0.5 to 0.5
Outputs:
- atom_energy: float32 [131072], P(('gx', 'gy'))
- forces: float32 [3, 131072], P(None, ('gx', 'gy'))
The draws below stay inside these ranges and needn't reach their ends.
Inputs may be any that keep to these rules, and one draw needn't show every extreme that they name: `tile_list`: row 0 of each slot names one of the device's own 8 blocks, row 1 a block of its node list (8 own blocks, then 2 ghost blocks); slot k < 2 of every device names ghost block 8 + k. The first counts slots of a device are live, the rest are ignored.
All inputs are finite; a program needn't handle non-finite values.
Results may differ from the reference program's by a relative error of at most 0.0003.
Values sent between devices are 32-bit elements; how exact they have to be, the bound alone decides.
A program may use at most 64 MiB of HBM per device.

```python
import jax
import jax.numpy as jnp
from jax import lax

CHANNELS = 128
RADIAL_BASIS = 8
ELEMENTS = 6
BLOCK_ATOMS = 64
LOCAL_BLOCKS = 8
GHOSTS = 16
TILE_SLOTS = 6
ATOMS_DEV = 512
GHOST_BLOCKS = 2
ATOMS = 131072
SEND_ROWS = 4096
TILES_ALL = 1536
N_GX = 64
N_GY = 4
DEVICES = 256


def draw_tile_list(key, part):
    slot_total = TILES_ALL
    first_key, second_key = jax.random.split(jax.random.fold_in(key, 3))
    left_block = jax.random.randint(first_key, (slot_total,), 0, LOCAL_BLOCKS, dtype=jnp.int32)
    slot_of = jnp.arange(slot_total, dtype=jnp.int32) % TILE_SLOTS
    anywhere = jax.random.randint(second_key, (slot_total,), 0, LOCAL_BLOCKS + GHOST_BLOCKS, dtype=jnp.int32)
    right_block = jnp.where(slot_of < GHOST_BLOCKS, LOCAL_BLOCKS + slot_of, anywhere)
    return jnp.stack([left_block, right_block]).astype(jnp.int32)


def draw_counts(key, part):
    device_total = DEVICES
    spread_key, busy_key, light_key = jax.random.split(jax.random.fold_in(key, 5), 3)
    slot_span = TILE_SLOTS - GHOST_BLOCKS
    spread = jax.random.randint(spread_key, (device_total,), 0, slot_span + 1, dtype=jnp.int32)
    live_counts = GHOST_BLOCKS + spread * spread // slot_span
    busiest = jax.random.randint(busy_key, (), 0, device_total, dtype=jnp.int32)
    lowest = (busiest + 1 + jax.random.randint(light_key, (), 0, device_total - 1, dtype=jnp.int32)) % device_total
    devices_at = jnp.arange(device_total, dtype=jnp.int32)
    live_counts = jnp.where(devices_at == busiest, TILE_SLOTS, jnp.where(devices_at == lowest, GHOST_BLOCKS, live_counts))
    return live_counts.astype(jnp.int32)


def with_ends(drawn, rng, low, high):
    longest = drawn.shape.index(max(drawn.shape))
    spots = []
    for shift in (0, 1):
        where = [jax.random.randint(jax.random.fold_in(rng, axis), (), 0, length) for axis, length in enumerate(drawn.shape)]
        where[longest] = (where[longest] + shift) % drawn.shape[longest]
        spots.append(tuple(where))
    return drawn.at[spots[0]].set(low).at[spots[1]].set(high)


def shard_levels(own_key, extent, cuts, low, largest):
    level = 1.0
    for position, shards_of in cuts:
        heights = jax.random.uniform(jax.random.fold_in(jax.random.fold_in(own_key, 6), position), (shards_of,), jnp.float32, low / len(cuts), largest / len(cuts))
        level = level * jnp.repeat(jnp.exp(heights), extent[position] // shards_of).reshape((-1,) + (1,) * (len(extent) - 1 - position))
    return level


def bell_draw(rng, extent, scale, reach, held_as=jnp.bfloat16):
    entries = jax.random.normal(rng, extent, jnp.float32) * scale
    return jnp.minimum(jnp.maximum(entries, -reach), reach).astype(held_as)


def setup_inputs(seed: int = 0) -> dict:
    keys = jax.random.split(jax.random.key(seed), 10)
    fractions = jnp.clip(1.0 * jax.random.uniform(keys[0], (3, ATOMS), jnp.float32) ** shard_levels(keys[0], (3, ATOMS), ((1, 256),), -0.2, 0.2), 0.0, 1.0)
    species = with_ends(jax.random.randint(keys[1], (ATOMS,), 0, ELEMENTS), jax.random.fold_in(keys[1], 1), 0, ELEMENTS - 1).astype(jnp.int32)
    send_list = with_ends(jax.random.randint(keys[2], (8, SEND_ROWS), 0, ATOMS_DEV), jax.random.fold_in(keys[2], 1), 0, ATOMS_DEV - 1).astype(jnp.int32)
    tile_list = draw_tile_list(jax.random.fold_in(keys[9], 71), 0)
    counts = draw_counts(jax.random.fold_in(keys[9], 71), 0)
    embedding = bell_draw(keys[5], (ELEMENTS, CHANNELS), 1.0, 6.0, jnp.float32)
    radial = bell_draw(keys[6], (4, RADIAL_BASIS, CHANNELS), BLOCK_ATOMS ** -0.5, 0.75, jnp.float32)
    mixing = bell_draw(keys[7], (5, CHANNELS, CHANNELS), CHANNELS ** -0.5, 0.5, jnp.float32)
    readout = bell_draw(keys[8], (CHANNELS,), CHANNELS ** -0.5, 0.5, jnp.float32)
    return {"fractions": fractions, "species": species, "send_list": send_list, "tile_list": tile_list, "counts": counts, "embedding": embedding, "radial": radial, "mixing": mixing, "readout": readout}


OFFSETS = ((-1, -1), (-1, 0), (-1, 1), (0, -1), (0, 1), (1, -1), (1, 0), (1, 1))
WIDTHS = (12.0, 12.0, 36.0)
CUTOFF = 5.0
SHARPNESS = 2.0
HIGHEST = lax.Precision.HIGHEST

def pair_terms(left_pos, right_pos, same_node):
    separation = right_pos[:, None, :] - left_pos[:, :, None]
    dist_sq = lax.optimization_barrier(jnp.sum(separation * separation, axis=0))
    softened = jnp.sqrt(dist_sq + 1.0)
    envelope = jnp.square(jnp.maximum(1.0 - dist_sq / (CUTOFF * CUTOFF), 0.0)) * (1.0 - same_node)
    centers = 1.0 + 0.6 * jnp.arange(RADIAL_BASIS, dtype=jnp.float32)
    radial_terms = envelope[None] * jnp.exp(-SHARPNESS * jnp.square(softened[None] - centers[:, None, None]))
    return (radial_terms, separation / softened[None])

def message_one(left_pos, right_pos, right_scalar, same_node, weight_scalar, weight_vector):
    radial_terms, direction = pair_terms(left_pos, right_pos, same_node)
    block_size = right_pos.shape[1]
    angular = jnp.concatenate([jnp.ones_like(direction[:1]), direction], axis=0)
    kernel = radial_terms[:, None] * angular[None]
    projected = jnp.dot(kernel.reshape(-1, block_size), right_scalar, precision=HIGHEST)
    projected = projected.reshape(radial_terms.shape[0], 4, left_pos.shape[1], right_scalar.shape[1])
    scalar_msg = jnp.einsum('nc,nic->ic', weight_scalar, projected[:, 0], precision=HIGHEST)
    vector_msg = jnp.einsum('nc,naic->aic', weight_vector, projected[:, 1:], precision=HIGHEST)
    return (scalar_msg, vector_msg)

def message_two(left_pos, right_pos, right_scalar, right_vector, same_node, weight_scalar, weight_vector):
    radial_terms, direction = pair_terms(left_pos, right_pos, same_node)
    basis_count = radial_terms.shape[0]
    row_count = left_pos.shape[1]
    block_size = right_pos.shape[1]
    from_scalar = jnp.dot(radial_terms.reshape(-1, block_size), right_scalar, precision=HIGHEST)
    from_scalar = from_scalar.reshape(basis_count, row_count, -1)
    kernel = radial_terms[:, :, None, :] * jnp.transpose(direction, (1, 0, 2))[None]
    from_vector = jnp.dot(kernel.reshape(basis_count * row_count, 3 * block_size), right_vector.reshape(3 * block_size, -1), precision=HIGHEST)
    from_vector = from_vector.reshape(basis_count, row_count, -1)
    return jnp.einsum('nc,nic->ic', weight_scalar, from_scalar, precision=HIGHEST) + jnp.einsum('nc,nic->ic', weight_vector, from_vector, precision=HIGHEST)

def add_rows(running, addend, offset, dimension):
    current = lax.dynamic_slice_in_dim(running, offset, addend.shape[dimension], dimension)
    return lax.dynamic_update_slice_in_dim(running, current + addend, offset, dimension)

def ghost_slots(table, send_grid):
    gathered = []
    for slot_index, (along_x, along_y) in enumerate(OFFSETS):
        chosen = send_grid[7 - slot_index]
        picked = jax.vmap(jax.vmap(lambda source, rows_at: source[rows_at]))(table, chosen)
        gathered.append(jnp.roll(picked, (-along_x, -along_y), axis=(0, 1)))
    return jnp.stack(gathered, axis=2)

def reference(fractions, species, send_list, tile_list, counts, embedding, radial, mixing, readout):
    device_total = N_GX * N_GY
    node_count = ATOMS_DEV + 8 * GHOSTS
    channels = embedding.shape[1]
    grid_frac = fractions.reshape(3, N_GX, N_GY, ATOMS_DEV)
    kind_grid = species.reshape(N_GX, N_GY, ATOMS_DEV)
    send_grid = send_list.reshape(8, N_GX, N_GY, GHOSTS)
    tile_grid = jnp.transpose(tile_list.reshape(2, device_total, TILE_SLOTS), (1, 0, 2))
    widths = jnp.array(WIDTHS, jnp.float32)
    shifts = jnp.array([[float(along_x), float(along_y), 0.0] for along_x, along_y in OFFSETS], jnp.float32)
    within = jnp.arange(BLOCK_ATOMS, dtype=jnp.int32)
    onehot = (kind_grid[..., None] == jnp.arange(ELEMENTS, dtype=jnp.int32)).astype(jnp.float32)
    local_embed = jnp.dot(onehot, embedding, precision=HIGHEST)
    ghost_embed = ghost_slots(local_embed, send_grid).reshape(N_GX, N_GY, 8 * GHOSTS, channels)
    all_embed = jnp.concatenate([local_embed, ghost_embed], axis=2).reshape(device_total, node_count, channels)

    def tile_view(tiles_here, tile_slot):
        left_start = tiles_here[0, tile_slot] * BLOCK_ATOMS
        right_start = tiles_here[1, tile_slot] * BLOCK_ATOMS
        same_node = ((left_start + within)[:, None] == (right_start + within)[None, :]).astype(jnp.float32)
        return (left_start, right_start, same_node)

    def layer_one_device(inputs_one):
        positions, scalars, tiles_here, live_count = inputs_one

        def advance(carried, tile_slot):
            scalar_acc, vector_acc = carried
            left_start, right_start, same_node = tile_view(tiles_here, tile_slot)
            left_pos = lax.dynamic_slice_in_dim(positions, left_start, BLOCK_ATOMS, 1)
            right_pos = lax.dynamic_slice_in_dim(positions, right_start, BLOCK_ATOMS, 1)
            right_scalar = lax.dynamic_slice_in_dim(scalars, right_start, BLOCK_ATOMS, 0)
            scalar_msg, vector_msg = jax.checkpoint(message_one)(left_pos, right_pos, right_scalar, same_node, radial[0], radial[1])
            live = (tile_slot < live_count).astype(jnp.float32)
            scalar_acc = add_rows(scalar_acc, live * scalar_msg, left_start, 0)
            vector_acc = add_rows(vector_acc, live * vector_msg, left_start, 1)
            return ((scalar_acc, vector_acc), None)
        initial = (jnp.zeros((ATOMS_DEV, channels), jnp.float32), jnp.zeros((3, ATOMS_DEV, channels), jnp.float32))
        result, _ = lax.scan(advance, initial, jnp.arange(TILE_SLOTS, dtype=jnp.int32))
        return result

    def layer_two_device(inputs_two):
        positions, features, tiles_here, live_count = inputs_two

        def advance(scalar_acc, tile_slot):
            left_start, right_start, same_node = tile_view(tiles_here, tile_slot)
            left_pos = lax.dynamic_slice_in_dim(positions, left_start, BLOCK_ATOMS, 1)
            right_pos = lax.dynamic_slice_in_dim(positions, right_start, BLOCK_ATOMS, 1)
            right_feat = lax.dynamic_slice_in_dim(features, right_start, BLOCK_ATOMS, 1)
            scalar_msg = jax.checkpoint(message_two)(left_pos, right_pos, right_feat[0], right_feat[1:], same_node, radial[2], radial[3])
            live = (tile_slot < live_count).astype(jnp.float32)
            return (add_rows(scalar_acc, live * scalar_msg, left_start, 0), None)
        result, _ = lax.scan(advance, jnp.zeros((ATOMS_DEV, channels), jnp.float32), jnp.arange(TILE_SLOTS, dtype=jnp.int32))
        return result

    def energies(grid_positions):
        atom_frac = jnp.moveaxis(grid_positions, 0, -1)
        ghost_frac = ghost_slots(atom_frac, send_grid) + shifts[:, None, :]
        local_cart = atom_frac * widths
        ghost_cart = (ghost_frac * widths).reshape(N_GX, N_GY, 8 * GHOSTS, 3)
        all_cart = jnp.concatenate([local_cart, ghost_cart], axis=2).reshape(device_total, node_count, 3)
        all_cart = jnp.transpose(all_cart, (0, 2, 1))
        scalar_one, vector_one = lax.map(jax.checkpoint(layer_one_device), (all_cart, all_embed, tile_grid, counts))
        own_embed = local_embed.reshape(device_total, ATOMS_DEV, channels)
        scalar_next = own_embed + jax.nn.silu(jnp.dot(scalar_one, mixing[0], precision=HIGHEST))
        gate_values = jax.nn.sigmoid(jnp.dot(scalar_one, mixing[2], precision=HIGHEST))
        vector_next = jnp.dot(vector_one, mixing[1], precision=HIGHEST) * gate_values[:, None]
        features = jnp.concatenate([scalar_next[:, None], vector_next], axis=1)
        feat_grid = jnp.moveaxis(features.reshape(N_GX, N_GY, 4, ATOMS_DEV, channels), 2, 3)
        ghost_feat = ghost_slots(feat_grid, send_grid).reshape(N_GX, N_GY, 8 * GHOSTS, 4, channels)
        all_feat = jnp.concatenate([feat_grid, ghost_feat], axis=2)
        all_feat = jnp.moveaxis(all_feat, 3, 2).reshape(device_total, 4, node_count, channels)
        scalar_two = lax.map(jax.checkpoint(layer_two_device), (all_cart, all_feat, tile_grid, counts))
        scalar_final = scalar_next + jax.nn.silu(jnp.dot(scalar_two, mixing[3], precision=HIGHEST))
        hidden = jax.nn.silu(jnp.dot(scalar_final, mixing[4], precision=HIGHEST))
        return jnp.dot(hidden, readout, precision=HIGHEST)
    energy, energy_pull = jax.vjp(energies, grid_frac)
    grad_frac, = energy_pull(jnp.ones_like(energy))
    forces = -(grad_frac / widths[:, None, None, None])
    return (energy.reshape(ATOMS), forces.reshape(3, ATOMS))
```

```python
import functools

import jax
import jax.numpy as jnp
from jax import lax
from jax.experimental import pallas as pl
from jax.experimental.pallas import tpu as pltpu
from jax.sharding import PartitionSpec as P

OFFSETS = ((-1, -1), (-1, 0), (-1, 1), (0, -1), (0, 1), (1, -1), (1, 0), (1, 1))
WIDTHS = (12.0, 12.0, 36.0)
F32 = jnp.float32
BF16 = jnp.bfloat16
MESH = pl.DeviceIdType.MESH

BLOCK = 64
OWN = 8
NODES = 10
SLOTS = 6
BASIS = 8
CH = 128
PAIRS = BASIS * BLOCK
SPACING = 0.6
SHARP = 2.0
CUT_SQ = 25.0
RATE = 2.0 * SHARP * SPACING
FALL = SHARP * SPACING * SPACING


def mm(a, b):
    return lax.dot_general(a, b, (((1,), (0,)), ((), ())), preferred_element_type=F32)


def mmt(a, b):
    return lax.dot_general(a, b, (((1,), (1,)), ((), ())), preferred_element_type=F32)


def tmm(a, b):
    return lax.dot_general(a, b, (((0,), (0,)), ((), ())), preferred_element_type=F32)


def split(x):
    hi = x.astype(BF16)
    return hi, (x - hi.astype(F32)).astype(BF16)


def split_rows(x):
    hi = x.astype(BF16).astype(F32)
    rest = x - hi
    mid = rest.astype(BF16).astype(F32)
    return jnp.concatenate([hi, mid, rest - mid], axis=0).astype(BF16)


def three(dot, a_hi, a_lo, b_hi, b_lo):
    return dot(a_hi, b_hi) + dot(a_lo, b_hi) + dot(a_hi, b_lo)


def sigmoid(x):
    return 1.0 / (1.0 + jnp.exp(-x))


def lanes(rows, width=128):
    return lax.broadcasted_iota(jnp.int32, (rows, width), 1)


def rows_of(rows, width=128):
    return lax.broadcasted_iota(jnp.int32, (rows, width), 0)


def halves(x):
    return x + pltpu.roll(x, BLOCK, 1)


def kernel(
    nx, ny,
    sites_ref, send_ref, tiles_ref, counts_ref, emb_ref, rad_ref, mix_ref, rd_ref,
    energy_ref, force_ref,
    selt_ref, psend_ref, parr_ref, nodes_ref, col_ref, col3_ref, emb8_ref, wx_ref, wxh_ref, wxl_ref,
    m3_ref, m4_ref, m3t_ref, m4t_ref, radc_ref,
    lh_ref, ll_ref, geo_ref, gslot_ref, gown_ref, gsend_ref, garr_ref,
    rh_ref, rl_ref, pre_ref, s1_ref, ms2s_ref, ms2_ref, d_ref, ds2_ref,
    drh_ref, drl_ref, dfs_ref, df_ref, gback_ref, gret_ref, dg_ref, x_ref,
    isum_ref, jsum_ref, fsend_ref, farr_ref,
    send_sem, recv_sem,
):
    me_x, me_y = lax.axis_index("gx"), lax.axis_index("gy")
    peers = [(lax.rem(me_x + nx + ox, nx), lax.rem(me_y + ny + oy, ny)) for ox, oy in OFFSETS]

    barrier = pltpu.get_barrier_semaphore()
    for peer in peers:
        pl.semaphore_signal(barrier, inc=1, device_id=peer, device_id_type=MESH)

    lane8 = lanes(8)
    row8 = rows_of(8)
    lane = lanes(BLOCK)
    low = lane < BLOCK

    sites = sites_ref[...]
    listed = sites_ref[4:5, 0:128]
    selt_ref[...] = (rows_of(512).astype(F32) == listed).astype(BF16)
    picked = mm(split_rows(sites), selt_ref[...])
    psend_ref[...] = picked[0:8] + picked[8:16] + picked[16:24]

    pl.semaphore_wait(barrier, 8)

    def exchange(number, source, target):
        copies = []
        for r in range(8):
            copy = pltpu.make_async_remote_copy(
                src_ref=source(r),
                dst_ref=target(7 - r),
                send_sem=send_sem.at[number, r],
                recv_sem=recv_sem.at[number, 7 - r],
                device_id=peers[r],
                device_id_type=MESH,
            )
            copy.start()
            copies.append(copy)
        return copies

    def arrive(copies):
        for copy in copies:
            copy.wait()

    first = exchange(0, lambda r: psend_ref, lambda r: parr_ref.at[r])

    def place(pair, tile):
        turned = pltpu.roll(tile, BLOCK, 1)
        nodes_ref[2 * pair] = jnp.where(lane8 < BLOCK, tile, turned)
        nodes_ref[2 * pair + 1] = jnp.where(lane8 < BLOCK, turned, tile)
        upright = tile.T
        col_ref[2 * pair] = upright[0:BLOCK]
        col_ref[2 * pair + 1] = upright[BLOCK:]

    for pair in range(4):
        place(pair, sites[:, 128 * pair : 128 * pair + 128])

    emb8_ref[...] = jnp.zeros((8, CH), F32)
    emb8_ref[0:6] = emb_ref[...]
    emb8 = emb8_ref[...]
    level = lax.broadcasted_iota(jnp.int32, (BASIS, CH), 0).astype(F32)
    fall = jnp.exp(-FALL * level * level)
    for path in range(4):
        radc_ref[path] = rad_ref[path] * fall
    w01 = jnp.concatenate(
        [emb8 * radc_ref[path, n : n + 1] for path in range(2) for n in range(BASIS)], axis=0
    )
    w_hi, w_lo = split(w01)
    wx_ref[...] = jnp.zeros_like(wx_ref)
    for matrix, row0, columns in ((0, 0, (0,)), (2, 0, (1,)), (1, 64, (2, 3, 4))):
        m_hi, m_lo = split(mix_ref[matrix])
        made = three(mm, w_hi[row0 : row0 + 64], w_lo[row0 : row0 + 64], m_hi, m_lo)
        for n in range(BASIS):
            for column in columns:
                comp = max(column - 1, 0)
                wx_ref[n * 32 + comp * 8 : n * 32 + comp * 8 + 8, column * CH : column * CH + CH] = made[
                    n * 8 : n * 8 + 8
                ]
    wx_hi, wx_lo = split(wx_ref[...])
    wxh_ref[...] = wx_hi
    wxl_ref[...] = wx_lo
    for matrix, straight, turned in ((3, m3_ref, m3t_ref), (4, m4_ref, m4t_ref)):
        m_hi, m_lo = split(mix_ref[matrix])
        straight[0:CH, 0:CH] = m_hi
        straight[0:CH, CH:] = m_lo
        straight[CH:, 0:CH] = m_hi
        straight[CH:, CH:] = jnp.zeros((CH, CH), BF16)
        turned[0:CH, 0:CH] = m_hi
        turned[0:CH, CH:] = m_hi
        turned[CH:, 0:CH] = m_lo
        turned[CH:, CH:] = jnp.zeros((CH, CH), BF16)
    e_hi = emb8.astype(BF16).astype(F32)
    e_rest = emb8 - e_hi
    e_mid = e_rest.astype(BF16).astype(F32)
    col3_ref[...] = jnp.concatenate(
        [e_hi, e_mid, e_rest - e_mid, jnp.zeros((CH - 24, CH), F32)], axis=0
    ).astype(BF16)

    def clear(b, _):
        rh_ref[b] = jnp.zeros((256, 256), BF16)
        rl_ref[b] = jnp.zeros((256, 256), BF16)
        return 0

    lax.fori_loop(0, NODES, clear, 0)

    arrive(first)
    group = lane8 // 16
    ghosts = jnp.zeros((8, 128), F32)
    for k in range(8):
        ghosts = jnp.where(group == k, pltpu.roll(parr_ref[k], (16 * (2 * k - 7)) % 128, 1), ghosts)
    off_x = jnp.where(group < 3, -1.0, jnp.where(group < 5, 0.0, 1.0))
    is_left = (group == 0) | (group == 3) | (group == 5)
    is_mid = (group == 1) | (group == 6)
    off_y = jnp.where(is_left, -1.0, jnp.where(is_mid, 0.0, 1.0))
    shift = jnp.where(row8 == 0, off_x * WIDTHS[0], jnp.where(row8 == 1, off_y * WIDTHS[1], 0.0))
    place(4, ghosts + shift)

    comp_of = (lane // 8) & 3
    kind_of = (lane & 7).astype(F32)

    def kinds(J):
        match = kind_of == col_ref[J][:, 3:4]
        return jnp.concatenate(
            [jnp.where(match & (comp_of == comp), 1.0, 0.0) for comp in range(4)], axis=0
        ).astype(BF16)

    def forward_one(k, _):
        I, J = tiles_ref[0, k], tiles_ref[1, k]
        at = col_ref[I]
        to = nodes_ref[J]
        r = [to[a : a + 1] - at[:, a : a + 1] for a in range(3)]
        d2 = r[0] * r[0] + r[1] * r[1] + r[2] * r[2]
        q = jnp.sqrt(d2 + 1.0)
        inv = 1.0 / q
        live = jnp.where(k < counts_ref[0], 1.0, 0.0)
        same = rows_of(BLOCK) + I * BLOCK == (lane & (BLOCK - 1)) + J * BLOCK
        m = jnp.where(same, 0.0, jnp.maximum(1.0 - d2 / CUT_SQ, 0.0)) * live
        t = jnp.minimum(q, 5.125) - 1.0
        e = jnp.exp(RATE * t)
        f = jnp.exp(-SHARP * t * t)
        u01 = jnp.where(low, 1.0, r[0] * inv)
        u23 = jnp.where(low, r[1], r[2]) * inv
        geo_ref[k, 0] = q
        geo_ref[k, 1] = inv
        geo_ref[k, 2] = m
        geo_ref[k, 3] = e
        geo_ref[k, 4] = f
        geo_ref[k, 5] = u01
        geo_ref[k, 6] = u23
        h = m * m * f
        for n in range(BASIS):
            here = pl.ds(n * BLOCK, BLOCK)
            for half, u in enumerate((u01, u23)):
                hi, lo = split(h * u)
                lh_ref[k, here, pl.ds(half * 128, 128)] = hi
                ll_ref[k, here, pl.ds(half * 128, 128)] = lo
            h = h * e
        chosen = kinds(J)
        out = mm(lh_ref[k], chosen) + mm(ll_ref[k], chosen)
        for half in range(2):
            merged = jnp.zeros((BLOCK, 128), F32)
            for n in range(4):
                row0 = (half * 4 + n) * BLOCK
                merged = jnp.where(lane // 32 == n, out[row0 : row0 + BLOCK], merged)
            gslot_ref[k, :, pl.ds(half * 128, 128)] = merged
        return 0

    lax.fori_loop(0, SLOTS, forward_one, 0)

    def hit(which, k, b):
        return jnp.where(tiles_ref[which, k] == b, 1.0, 0.0)

    def gather_one(b, _):
        total = hit(0, 0, b) * gslot_ref[0]
        for k in range(1, SLOTS):
            total += hit(0, k, b) * gslot_ref[k]
        gown_ref[pl.ds(pl.multiple_of(b * BLOCK, BLOCK), BLOCK)] = total
        return 0

    lax.fori_loop(0, OWN, gather_one, 0)

    for g in range(128):
        gsend_ref[g : g + 1] = gown_ref[pl.ds(send_ref[g // 16, g % 16], 1)]
    second = exchange(
        1, lambda r: gsend_ref.at[pl.ds(16 * r, 16)], lambda r: garr_ref.at[pl.ds(16 * r, 16)]
    )

    def features(first_block, blocks, sums, own):
        count = blocks * BLOCK
        row0 = pl.multiple_of(first_block * BLOCK, BLOCK)
        g_hi, g_lo = split(sums)
        pre = three(mm, g_hi, g_lo, wxh_ref[...], wxl_ref[...])
        pre_ref[pl.ds(row0, count)] = pre
        wide = lanes(count)
        kind = jnp.concatenate([col_ref[first_block + b][:, 3:4] for b in range(blocks)], axis=0)
        pick = jnp.where(((wide & 7).astype(F32) == kind) & (wide < 24), 1.0, 0.0).astype(BF16)
        start = mm(pick, col3_ref[...])
        raw = pre[:, 0:CH]
        s1 = start + raw * sigmoid(raw)
        gate = sigmoid(pre[:, CH : 2 * CH])
        if own:
            s1_ref[pl.ds(row0, count)] = s1
        parts = [split(s1)] + [split(pre[:, (2 + a) * CH : (3 + a) * CH] * gate) for a in range(3)]
        for b in range(blocks):
            for comp, (hi, lo) in enumerate(parts):
                column = 0 if comp == 0 else CH
                spot = (first_block + b, pl.ds(comp * BLOCK, BLOCK), pl.ds(column, CH))
                rh_ref[spot] = hi[b * BLOCK : b * BLOCK + BLOCK]
                rl_ref[spot] = lo[b * BLOCK : b * BLOCK + BLOCK]

    def features_own(i, _):
        features(i * 4, 4, gown_ref[pl.ds(pl.multiple_of(i * 256, 256), 256)], True)
        return 0

    lax.fori_loop(0, 2, features_own, 0)
    arrive(second)
    features(8, 2, garr_ref[...], False)

    def forward_two(k, _):
        J = tiles_ref[1, k]
        out = three(mm, lh_ref[k], ll_ref[k], rh_ref[J], rl_ref[J])
        total = jnp.zeros((BLOCK, CH), F32)
        for n in range(BASIS):
            part = out[n * BLOCK : n * BLOCK + BLOCK]
            total += part[:, 0:CH] * radc_ref[2, n : n + 1] + part[:, CH:] * radc_ref[3, n : n + 1]
        ms2s_ref[k] = total
        return 0

    lax.fori_loop(0, SLOTS, forward_two, 0)

    def gather_two(b, _):
        total = hit(0, 0, b) * ms2s_ref[0]
        for k in range(1, SLOTS):
            total += hit(0, k, b) * ms2s_ref[k]
        ms2_ref[pl.ds(pl.multiple_of(b * BLOCK, BLOCK), BLOCK)] = total
        return 0

    lax.fori_loop(0, OWN, gather_two, 0)

    rd = rd_ref[...]
    rd_rows = split_rows(jnp.broadcast_to(rd, (8, CH)))

    def packed(dot, x, w):
        hi, lo = split(x)
        both = dot(jnp.concatenate([hi, lo], axis=1), w)
        return both[:, 0:CH] + both[:, CH:]

    def finish(i):
        here = pl.ds(i * 256, 256)
        z3 = packed(mm, ms2_ref[here], m3_ref[...])
        g3 = sigmoid(z3)
        s2 = s1_ref[here] + z3 * g3
        z4 = packed(mm, s2, m4_ref[...])
        g4 = sigmoid(z4)
        h_hi, h_lo = split(z4 * g4)
        e_a = mmt(rd_rows, h_hi)
        e_b = mmt(rd_rows, h_lo)
        e_all = e_a[0:8] + e_a[8:16] + e_a[16:24] + e_b[0:8] + e_b[8:16]
        energy_ref[:, here] = e_all[0:1]
        dz4 = rd * (g4 + z4 * g4 * (1.0 - g4))
        ds2 = packed(mmt, dz4, m4t_ref[...])
        dz3 = ds2 * (g3 + z3 * g3 * (1.0 - g3))
        dm = packed(mmt, dz3, m3t_ref[...])
        ds2_ref[here] = ds2
        for b in range(4):
            d_ref[i * 4 + b] = dm[b * BLOCK : b * BLOCK + BLOCK]

    for i in range(2):
        finish(i)

    def backward_two(k, _):
        D = d_ref[tiles_ref[0, k]]
        for n in range(BASIS):
            for half in range(2):
                hi, lo = split(D * radc_ref[2 + half, n : n + 1])
                drh_ref[k, pl.ds(n * BLOCK, BLOCK), pl.ds(half * CH, CH)] = hi
                drl_ref[k, pl.ds(n * BLOCK, BLOCK), pl.ds(half * CH, CH)] = lo
        out = three(tmm, lh_ref[k], ll_ref[k], drh_ref[k], drl_ref[k])
        dfs_ref[k, 0:BLOCK] = out[0:BLOCK, 0:CH]
        dfs_ref[k, BLOCK:] = out[BLOCK:, CH:]
        return 0

    lax.fori_loop(0, SLOTS, backward_two, 0)

    def gather_right(b, first_slot, part):
        total = hit(1, first_slot, b) * dfs_ref[first_slot, part]
        for k in range(first_slot + 1, SLOTS):
            total += hit(1, k, b) * dfs_ref[k, part]
        return total

    for b in range(2):
        df_ref[OWN + b] = gather_right(OWN + b, 0, pl.ds(0, 256))

    def pull(first_block, blocks, extra):
        count = blocks * BLOCK
        row0 = pl.multiple_of(first_block * BLOCK, BLOCK)
        pre = pre_ref[pl.ds(row0, count)]

        def part(comp):
            return jnp.concatenate(
                [df_ref[first_block + b, pl.ds(comp * BLOCK, BLOCK)] for b in range(blocks)], axis=0
            )

        raw = pre[:, 0:CH]
        g = sigmoid(raw)
        d_scalar = part(0) if extra is None else part(0) + extra
        d_raw = d_scalar * (g + raw * g * (1.0 - g))
        gate = sigmoid(pre[:, CH : 2 * CH])
        d_vec = [part(1 + a) for a in range(3)]
        d_gate = d_vec[0] * pre[:, 2 * CH : 3 * CH]
        for a in range(1, 3):
            d_gate += d_vec[a] * pre[:, (2 + a) * CH : (3 + a) * CH]
        d_gate = d_gate * (gate * (1.0 - gate))
        d_pre = jnp.concatenate([d_raw, d_gate] + [d * gate for d in d_vec], axis=1)
        p_hi, p_lo = split(d_pre)
        return three(mmt, p_hi, p_lo, wxh_ref[...], wxl_ref[...])

    gback_ref[...] = pull(8, 2, None)
    third = exchange(
        2, lambda r: gback_ref.at[pl.ds(16 * r, 16)], lambda r: gret_ref.at[pl.ds(16 * r, 16)]
    )

    def gather_own(b, _):
        df_ref[b] = gather_right(b, 2, pl.ds(0, 256))
        return 0

    lax.fori_loop(0, OWN, gather_own, 0)

    def pull_own(i, _):
        here = pl.ds(pl.multiple_of(i * 256, 256), 256)
        made = pull(i * 4, 4, ds2_ref[here])
        for b in range(4):
            dg_ref[i * 4 + b] = made[b * BLOCK : b * BLOCK + BLOCK]
        return 0

    lax.fori_loop(0, 2, pull_own, 0)

    def pair_two(k, _):
        J = tiles_ref[1, k]
        x_ref[k] = three(mmt, drh_ref[k], drl_ref[k], rh_ref[J], rl_ref[J])
        return 0

    lax.fori_loop(0, SLOTS, pair_two, 0)

    arrive(third)
    back_hi, back_lo = split(gret_ref[...])
    back = jnp.concatenate([back_hi, back_lo], axis=0)
    selt = selt_ref[...]
    added = mm(jnp.concatenate([selt, selt], axis=1), back)
    for b in range(OWN):
        dg_ref[b] += added[b * BLOCK : b * BLOCK + BLOCK]

    ends = jnp.where((row8 == 0) == (lane8 < BLOCK), 1.0, 0.0).astype(F32)
    ends = jnp.concatenate([ends, ends], axis=1).astype(BF16)

    def backward_positions(k, _):
        J = tiles_ref[1, k]
        g_hi, g_lo = split(dg_ref[tiles_ref[0, k]])
        left = []
        none = jnp.zeros((BLOCK, 128), BF16)
        for n in range(BASIS):
            mine = lane // 32 == n % 4
            column = (n // 4) * 128
            left.append(
                jnp.concatenate(
                    [
                        jnp.where(mine, g_hi[:, column : column + 128], none),
                        jnp.where(mine, g_lo[:, column : column + 128], none),
                    ],
                    axis=1,
                )
            )
        chosen = kinds(J)
        x = x_ref[k] + mmt(
            jnp.concatenate(left, axis=0), jnp.concatenate([chosen, chosen], axis=1)
        )
        q, inv, m, e, f = (geo_ref[k, i] for i in range(5))
        u01, u23 = geo_ref[k, 5], geo_ref[k, 6]
        values, slopes = [], []
        for half in range(2):
            column = half * 128
            value = x[7 * BLOCK : 8 * BLOCK, column : column + 128]
            slope = jnp.zeros((BLOCK, 128), F32)
            for n in range(BASIS - 2, -1, -1):
                slope = slope * e + value
                value = value * e + x[n * BLOCK : n * BLOCK + BLOCK, column : column + 128]
            values.append(value * f)
            slopes.append(slope * (f * e))
        total = halves(u01 * values[0] + u23 * values[1])
        plain = halves(jnp.where(low, values[0], 0.0))
        rising = halves(u01 * slopes[0] + u23 * slopes[1])
        along = total - plain
        t = jnp.minimum(q, 5.125) - 1.0
        m2 = m * m
        radial = (-4.0 / CUT_SQ) * m * q * total + m2 * (RATE * rising - 2.0 * SHARP * t * total)
        factor = radial - m2 * inv * along
        scale = m2 * inv
        f01 = factor * u01 + scale * values[0]
        f23 = factor * u23 + scale * values[1]
        jsum_ref[k, 0:1] = jnp.sum(f01, axis=0, keepdims=True)
        jsum_ref[k, 1:2] = jnp.sum(f23, axis=0, keepdims=True)
        hi, lo = split(jnp.concatenate([f01, f23], axis=0))
        isum_ref[k] = mmt(ends, jnp.concatenate([hi, lo], axis=1))
        return 0

    lax.fori_loop(0, SLOTS, backward_positions, 0)

    def corner(b, first_slot, own):
        right = hit(1, first_slot, b) * jsum_ref[first_slot]
        for k in range(first_slot + 1, SLOTS):
            right += hit(1, k, b) * jsum_ref[k]
        right_turned = pltpu.roll(right, BLOCK, 1)
        along_x, along_y, along_z = right_turned[0:1], right[1:2], right_turned[1:2]
        if own:
            left = hit(0, 0, b) * isum_ref[0]
            for k in range(1, SLOTS):
                left += hit(0, k, b) * isum_ref[k]
            left_turned = pltpu.roll(left, BLOCK, 1)
            along_x -= left[1:2]
            along_y -= left_turned[0:1]
            along_z -= left_turned[1:2]
        return jnp.where(row8 == 0, along_x, jnp.where(row8 == 1, along_y, along_z))

    def pair_up(even, odd):
        return jnp.where(lane8 < BLOCK, even, pltpu.roll(odd, BLOCK, 1))

    fsend_ref[...] = pair_up(corner(8, 0, False), corner(9, 0, False))
    fourth = exchange(3, lambda r: fsend_ref, lambda r: farr_ref.at[r])
    own_tiles = [pair_up(corner(2 * p, 2, True), corner(2 * p + 1, 2, True)) for p in range(4)]
    arrive(fourth)
    returned = jnp.zeros((8, 128), F32)
    for k in range(8):
        returned = jnp.where(
            group == k, pltpu.roll(farr_ref[k], (16 * (2 * k - 7)) % 128, 1), returned
        )
    spread = mmt(split_rows(returned), selt_ref[...])
    spread = spread[0:8] + spread[8:16] + spread[16:24]
    for p in range(4):
        here = pl.ds(128 * p, 128)
        force_ref[:, here] = -(own_tiles[p] + spread[:, 128 * p : 128 * p + 128])[0:3]


def shards(nx, ny, fractions, species, send_list, tile_list, counts, embedding, radial, mixing, readout):
    widths = jnp.array(WIDTHS, F32)[:, None]
    sites = jnp.concatenate(
        [
            fractions * widths,
            species.astype(F32)[None],
            jnp.pad(send_list.reshape(1, 128).astype(F32), ((0, 0), (0, 384))),
            jnp.zeros((3, 512), F32),
        ],
        axis=0,
    )
    vmem = pl.BlockSpec(memory_space=pltpu.VMEM)
    smem = pl.BlockSpec(memory_space=pltpu.SMEM)
    V = pltpu.VMEM
    scratch = [
        V((512, 128), BF16),
        V((8, 128), F32),
        V((8, 8, 128), F32),
        V((NODES, 8, 128), F32),
        V((NODES, BLOCK, 8), F32),
        V((128, 128), BF16),
        V((8, 128), F32),
        V((256, 640), F32),
        V((256, 640), BF16),
        V((256, 640), BF16),
        V((256, 256), BF16),
        V((256, 256), BF16),
        V((256, 256), BF16),
        V((256, 256), BF16),
        V((4, BASIS, 128), F32),
        V((SLOTS, PAIRS, 256), BF16),
        V((SLOTS, PAIRS, 256), BF16),
        V((SLOTS, 7, BLOCK, 128), F32),
        V((SLOTS, BLOCK, 256), F32),
        V((512, 256), F32),
        V((128, 256), F32),
        V((128, 256), F32),
        V((NODES, 256, 256), BF16),
        V((NODES, 256, 256), BF16),
        V((640, 640), F32),
        V((512, 128), F32),
        V((SLOTS, BLOCK, 128), F32),
        V((512, 128), F32),
        V((OWN, BLOCK, 128), F32),
        V((512, 128), F32),
        V((SLOTS, PAIRS, 256), BF16),
        V((SLOTS, PAIRS, 256), BF16),
        V((SLOTS, 256, 128), F32),
        V((NODES, 256, 128), F32),
        V((128, 256), F32),
        V((128, 256), F32),
        V((OWN, BLOCK, 256), F32),
        V((SLOTS, PAIRS, 256), F32),
        V((SLOTS, 8, 128), F32),
        V((SLOTS, 8, 128), F32),
        V((8, 128), F32),
        V((8, 8, 128), F32),
        pltpu.SemaphoreType.DMA((4, 8)),
        pltpu.SemaphoreType.DMA((4, 8)),
    ]
    energy, forces = pl.pallas_call(
        functools.partial(kernel, nx, ny),
        out_shape=(
            jax.ShapeDtypeStruct((1, 512), F32),
            jax.ShapeDtypeStruct((3, 512), F32),
        ),
        in_specs=[vmem, smem, smem, smem, vmem, vmem, vmem, vmem],
        out_specs=(vmem, vmem),
        scratch_shapes=scratch,
        compiler_params=pltpu.CompilerParams(
            collective_id=0, has_side_effects=True, vmem_limit_bytes=48 * 1024 * 1024
        ),
        name="potential",
    )(sites, send_list, tile_list, counts, embedding, radial, mixing, readout.reshape(1, 128))
    return energy.reshape(512), forces


def solution(mesh):
    placed = (
        P(None, ("gx", "gy")),
        P(("gx", "gy")),
        P(None, ("gx", "gy")),
        P(None, ("gx", "gy")),
        P(("gx", "gy")),
        P(),
        P(),
        P(),
        P(),
    )
    return jax.shard_map(
        functools.partial(shards, mesh.shape["gx"], mesh.shape["gy"]),
        mesh=mesh,
        in_specs=placed,
        out_specs=(P(("gx", "gy")), P(None, ("gx", "gy"))),
        check_vma=False,
    )
```
